32 devices in a mesh: brick: 8 (over z, y), vec: 4 (over x, core).
Axes of the slice: x: 2, y: 2, z: 4, core: 2. Of those that a mesh axis runs over, the one named last changes fastest.
Arguments:
- right_side: float32 [4, 4, 32, 128, 128], P('vec', None, 'brick'), may hold values from -6 to 6
- diffusivity: float32 [32, 128, 128], P('brick'), may hold values from 0.3 to 3
Outputs:
- precond: float32 [4, 4, 32, 128, 128], P('vec', None, 'brick')
- gram: float32 [4, 4], P('vec')
The draws below stay inside these ranges and needn't reach their ends.
All inputs are finite; a program needn't handle non-finite values.
Results may differ from the reference program's by a relative error of at most 0.0003.
Values may be sent and summed in bfloat16 or wider, within the bound.
A program may use at most 64 MiB of HBM per device.

```python
import math
import jax
import jax.numpy as jnp
from jax import lax

FIELDS = 4
NY = 128
NZ = 128
SWEEPS = 6
NX = 32
VECS = 4


def draw_right_side(key, part):
    key_common = jax.random.fold_in(key, 11)
    key_mixing = jax.random.fold_in(key, 12)
    key_private = jax.random.fold_in(key, 13)
    full_shape = (VECS, FIELDS, NX, NY, NZ)
    mixing = 0.6 * jax.random.normal(key_mixing, (VECS, 3), jnp.float32)
    private_part = 0.7 * jax.random.normal(key_private, full_shape, jnp.float32)
    combined = private_part
    for component in range(3):
        common = jax.random.normal(jax.random.fold_in(key_common, component), (FIELDS, NX, NY, NZ), jnp.float32)
        combined = combined + mixing[:, component][:, None, None, None, None] * common[None]
    return jnp.clip(combined, -6.0, 6.0)


def block_scale(stream_key, extent, split, least, largest):
    def one(axis_at, blocks):
        heights = jax.random.uniform(jax.random.fold_in(jax.random.fold_in(stream_key, 6), axis_at), (blocks,), jnp.float32, least / len(split), largest / len(split))
        return jnp.repeat(jnp.exp(heights), extent[axis_at] // blocks).reshape((-1,) + (1,) * (len(extent) - axis_at - 1))

    loudness = one(*split[0])
    for cut in split[1:]:
        loudness = loudness * one(*cut)
    return loudness


def setup_inputs(seed: int = 0) -> dict:
    splits = jax.random.split(jax.random.key(seed), 3)
    return {
        "right_side": draw_right_side(jax.random.fold_in(splits[2], 71), 0),
        "diffusivity": jnp.clip(jnp.exp(math.log(3.0) - 2.3025851 * jax.random.uniform(splits[1], (NX, NY, NZ), jnp.float32) ** block_scale(splits[1], (NX, NY, NZ), ((0, 8),), -0.2, 0.2)), 0.3, 3.0),
    }


shift_value = 0.1
damping = 0.8


def pad_planes(field):
    widths = [(0, 0)] * (field.ndim - 3) + [(1, 1), (0, 0), (0, 0)]
    return jnp.pad(field, widths)


def neighbours(padded):
    middle = padded[..., 1:-1, :, :]
    total = padded[..., 2:, :, :] + padded[..., :-2, :, :]
    lead = [(0, 0)] * (middle.ndim - 2)
    side_y = jnp.pad(middle, lead + [(1, 1), (0, 0)])
    total = total + side_y[..., 2:, :] + side_y[..., :-2, :]
    side_z = jnp.pad(middle, lead + [(0, 0), (1, 1)])
    total = total + side_z[..., 2:] + side_z[..., :-2]
    return total


def operate(padded, kappa, scale):
    middle = padded[..., 1:-1, :, :]
    return shift_value * middle + scale * kappa * (6.0 * middle - neighbours(padded))


def pair_table(cols):
    fine = jnp.arange(cols, dtype=jnp.int32)
    coarse = jnp.arange(cols // 2, dtype=jnp.int32)
    return jnp.where(fine[:, None] // 2 == coarse[None, :], 1.0, 0.0).astype(jnp.float32)


def restrict(field):
    cols = field.shape[-1]
    summed = field[..., 0::2, :, :] + field[..., 1::2, :, :]
    summed = summed[..., 0::2, :] + summed[..., 1::2, :]
    halved = jnp.dot(summed, pair_table(cols), precision=lax.Precision.HIGHEST, preferred_element_type=jnp.float32)
    return halved * 0.125


def prolong(field):
    lead = field.shape[:-3]
    planes, rows, cols = field.shape[-3:]
    table = pair_table(2 * cols).T
    wide_cols = jnp.dot(field, table, precision=lax.Precision.HIGHEST, preferred_element_type=jnp.float32)
    wide = jnp.broadcast_to(wide_cols[..., :, None, :, None, :], lead + (planes, 2, rows, 2, 2 * cols))
    return wide.reshape(lead + (planes * 2, rows * 2, cols * 2))


def vcycle(right, kappa0):
    kappa1 = restrict(kappa0)
    kappa2 = restrict(kappa1)
    diag0 = shift_value + 6.0 * kappa0
    diag1 = shift_value + 6.0 * 0.25 * kappa1
    diag2 = shift_value + 6.0 * 0.0625 * kappa2
    level0 = damping * right / diag0
    resid0 = right - operate(pad_planes(level0), kappa0, 1.0)
    right1 = restrict(resid0)
    level1 = damping * right1 / diag1
    resid1 = right1 - operate(pad_planes(level1), kappa1, 0.25)
    right2 = restrict(resid1)
    level2 = damping * right2 / diag2
    for sweep in range(SWEEPS - 1):
        level2 = level2 + damping * (right2 - operate(pad_planes(level2), kappa2, 0.0625)) / diag2
    level1 = level1 + prolong(level2)
    level1 = level1 + damping * (right1 - operate(pad_planes(level1), kappa1, 0.25)) / diag1
    level0 = level0 + prolong(level1)
    level0 = level0 + damping * (right - operate(pad_planes(level0), kappa0, 1.0)) / diag0
    return level0


def reference(right_side, diffusivity):
    precond = lax.map(lambda right: vcycle(right, diffusivity), right_side)
    flat = precond.astype(jnp.bfloat16).reshape(right_side.shape[0], -1)
    gram = jnp.dot(flat, flat.T, preferred_element_type=jnp.float32)
    return precond, gram
```

```python
import functools

import jax
import jax.numpy as jnp
from jax import lax
from jax.experimental import pallas as pl
from jax.experimental.pallas import tpu as pltpu
from jax.sharding import PartitionSpec as P

SWEEPS = 6
shift_value = 0.1
damping = 0.8
keep = 1.0 - damping
F32 = jnp.float32
BF16 = jnp.bfloat16
MESH = pl.DeviceIdType.MESH


def rolled_sides(x, axis, width):
    size = x.shape[axis]
    place = lax.broadcasted_iota(jnp.int32, x.shape, axis) % width
    low = jnp.where(place == 0, 0.0, pltpu.roll(x, 1, axis))
    high = jnp.where(place == width - 1, 0.0, pltpu.roll(x, size - 1, axis))
    return low + high


def in_plane(x, width):
    return rolled_sides(x, 0, x.shape[0]) + rolled_sides(x, 1, width)


def split_dot(x, table):
    head = x.astype(BF16)
    tail = (x - head.astype(F32)).astype(BF16)
    return jnp.dot(head, table, preferred_element_type=F32) + jnp.dot(
        tail, table, preferred_element_type=F32
    )


def merge_table(parts, lanes):
    row = lax.broadcasted_iota(jnp.int32, (parts * lanes, lanes), 0)
    col = lax.broadcasted_iota(jnp.int32, (parts * lanes, lanes), 1)
    return jnp.where(row // 2 == col, 1.0, 0.0).astype(BF16)


def spread_table(parts, lanes):
    row = lax.broadcasted_iota(jnp.int32, (lanes, parts * lanes), 0)
    col = lax.broadcasted_iota(jnp.int32, (lanes, parts * lanes), 1)
    return jnp.where(col // 2 == row, 1.0, 0.0).astype(BF16)


def repeat_table(lanes, source, width):
    row = lax.broadcasted_iota(jnp.int32, (lanes, lanes), 0)
    col = lax.broadcasted_iota(jnp.int32, (lanes, lanes), 1)
    hit = (row // 2 == col % width) & (row < source)
    return jnp.where(hit, 1.0, 0.0).astype(BF16)


def kernel(bricks, group, reach, rhs, kap, out, gram, xp, g0, x0s, x0h, tmp, ktmp, x1p, x1s,
           x1h, b1s, k1s, q1s, q1h, t1, x2s, x2h, q2s, q2h, t2, w1, w0, zb, zr, part, g1h, rows_s,
           g2h, sems_r, sems_s):
    fields, planes, ys, zs = rhs.shape[1:]
    pairs = fields // 2
    y1, y2 = ys // 2, ys // 4
    width1, width2 = zs // 2, zs // 4
    half = planes // 2
    b = lax.axis_index("brick")
    v = lax.axis_index("vec")
    has = (b > 0, b < bricks - 1)
    side = (-1, 1)
    counter = [0]
    sends = []

    def copy(src, dst, sem, brick, vec):
        return pltpu.make_async_remote_copy(
            src_ref=src, dst_ref=dst, send_sem=sems_s.at[sem], recv_sem=sems_r.at[sem],
            device_id=(brick, vec), device_id_type=MESH)

    def begin(cond, src, dst, sem, brick, vec):
        made = copy(src, dst, sem, brick, vec)
        if cond is None:
            made.start()
        else:
            pl.when(cond)(made.start)
        sends.append((cond, made))

    def arrive(cond, dst, sem):
        waiter = copy(dst, dst, sem, b, v)
        if cond is None:
            waiter.wait_recv()
        else:
            pl.when(cond)(waiter.wait_recv)

    def number(count):
        base = counter[0]
        counter[0] += count
        return base

    sem_x0 = number(2 * fields)
    sem_x1 = number(4)
    sem_q1 = number(2)
    sem_x2 = number(2 * reach + 1)
    sem_q2 = number(2 * reach + 1)
    sem_z = number(group)
    sem_g1 = number(group)
    sem_g2 = number(bricks)

    barrier = pltpu.get_barrier_semaphore()
    for step in range(1, bricks):
        pl.semaphore_signal(barrier, inc=1, device_id=((b + step) % bricks, v),
                            device_id_type=MESH)
    for step in range(1, group):
        pl.semaphore_signal(barrier, inc=1, device_id=(b, (v + step) % group),
                            device_id_type=MESH)

    for p in range(planes):
        g0[p] = damping / (shift_value + 6.0 * kap[p])
    for f in range(fields):
        for p in range(planes):
            x = g0[p] * rhs[0, f, p]
            xp[f, p + 1] = x
            if p == 0:
                x0s[0, f] = x.astype(BF16)
            if p == planes - 1:
                x0s[1, f] = x.astype(BF16)
    for s in range(2):
        @pl.when(jnp.logical_not(has[s]))
        def _(s=s):
            x0h[s] = jnp.zeros_like(x0h.at[s])
            x1h[s] = jnp.zeros_like(x1h.at[s])
            q1h[s] = jnp.zeros_like(q1h.at[s])
    for off in range(-reach, reach + 1):
        if off:
            @pl.when((b + off < 0) | (b + off >= bricks))
            def _(off=off):
                x2h[off + reach] = jnp.zeros_like(x2h.at[off + reach])
                q2h[off + reach] = jnp.zeros_like(q2h.at[off + reach])

    pl.semaphore_wait(barrier, bricks - 1 + group - 1)
    for f in range(fields):
        for s in range(2):
            begin(has[s], x0s.at[s, f], x0h.at[1 - s, f], sem_x0 + (1 - s) * fields + f,
                  b + side[s], v)

    merge = merge_table(2, zs)
    spread = spread_table(2, zs)
    for h in range(half):
        ktmp[h] = kap[2 * h] + kap[2 * h + 1]
    k1 = []
    for h in range(half):
        summed = ktmp.at[h][pl.ds(0, y1, stride=2), :] + ktmp.at[h][pl.ds(1, y1, stride=2), :]
        k = split_dot(summed, repeat_table(zs, zs, width1)) * 0.125
        k1s[h] = k
        k1.append(k)
    gd1 = [damping / (shift_value + 6.0 * 0.25 * k) for k in k1]
    for h in range(half):
        q1s[h] = gd1[h] * (0.25 * k1[h])
    t1[0] = k1[0] + k1[1]
    summed = t1.at[0][pl.ds(0, y2, stride=2), :] + t1.at[0][pl.ds(1, y2, stride=2), :]
    k2 = split_dot(summed, repeat_table(zs, width1, width2)) * 0.125
    gd2 = damping / (shift_value + 6.0 * 0.0625 * k2)
    q2s[...] = gd2 * (0.0625 * k2)
    for s in range(2):
        begin(has[s], q1s.at[0 if s == 0 else half - 1], q1h.at[1 - s], sem_q1 + 1 - s,
              b + side[s], v)
    for size in range(1, reach + 1):
        for off in (-size, size):
            begin((b + off >= 0) & (b + off < bricks), q2s, q2h.at[reach - off],
                  sem_q2 + reach - off, b + off, v)

    for pair in range(pairs):
        halved = [[None] * 2 for _ in range(half)]
        for inner in range(2):
            f = 2 * pair + inner
            for s in range(2):
                arrive(has[s], x0h.at[s, f], sem_x0 + s * fields + f)
            xp[f, 0] = x0h[0, f].astype(F32)
            xp[f, planes + 1] = x0h[1, f].astype(F32)
            for h in range(half):
                total = None
                for p in (2 * h, 2 * h + 1):
                    around = in_plane(xp[f, p + 1], zs) + xp[f, p] + xp[f, p + 2]
                    resid = keep * rhs[0, f, p] + kap[p] * around
                    total = resid if total is None else total + resid
                tmp[f, h] = total
                view = tmp.at[f, h]
                halved[h][inner] = view[pl.ds(0, y1, stride=2), :] + view[pl.ds(1, y1, stride=2), :]
        for h in range(half):
            b1 = split_dot(jnp.concatenate(halved[h], axis=1), merge) * 0.125
            b1s[pair, h] = b1
            x1 = gd1[h] * b1
            x1p[pair, h + 2] = x1
            x1s[h, pair] = x1.astype(x1s.dtype)

    for order in range(half):
        for s in range(2):
            plane = order if s == 0 else half - 1 - order
            begin(has[s], x1s.at[plane], x1h.at[1 - s, order], sem_x1 + (1 - s) * 2 + order,
                  b + side[s], v)
    for s in range(2):
        arrive(has[s], x1h.at[s, 0], sem_x1 + s * 2)
    halved = []
    for pair in range(pairs):
        x1p[pair, 1] = x1h[0, 0, pair].astype(F32)
        x1p[pair, half + 2] = x1h[1, 0, pair].astype(F32)
        total = None
        for h in range(half):
            around = in_plane(x1p[pair, h + 2], width1) + x1p[pair, h + 1] + x1p[pair, h + 3]
            resid = keep * b1s[pair, h] + 0.25 * k1s[h] * around
            total = resid if total is None else total + resid
        t1[pair] = total
        view = t1.at[pair]
        halved.append(view[pl.ds(0, y2, stride=2), :] + view[pl.ds(1, y2, stride=2), :])
    b2 = split_dot(jnp.concatenate(halved, axis=1), merge) * 0.125
    x20 = gd2 * b2
    x2s[...] = x20.astype(x2s.dtype)
    for size in range(reach, 0, -1):
        for off in (-size, size):
            begin((b + off >= 0) & (b + off < bricks), x2s, x2h.at[reach - off],
                  sem_x2 + reach - off, b + off, v)
    for s in range(2):
        arrive(has[s], x1h.at[s, 1], sem_x1 + s * 2 + 1)
        arrive(has[s], q1h.at[s], sem_q1 + s)
        for pair in range(pairs):
            x1p[pair, 0 if s == 0 else half + 3] = x1h[s, 1, pair].astype(F32)
    for off in range(-reach, reach + 1):
        if off:
            cond = (b + off >= 0) & (b + off < bricks)
            arrive(cond, q2h.at[off + reach], sem_q2 + off + reach)
            arrive(cond, x2h.at[off + reach], sem_x2 + off + reach)

    start = {off: x2h[off + reach].astype(F32) for off in range(-reach, reach + 1) if off}
    start[0] = x20
    level2 = dict(start)
    zero = jnp.zeros_like(x20)
    for sweep in range(1, SWEEPS):
        wide = SWEEPS - sweep
        after = {}
        for off in range(-min(wide, reach), min(wide, reach) + 1):
            x = level2[off]
            around = in_plane(x, width2) + level2.get(off - 1, zero) + level2.get(off + 1, zero)
            coeff = q2s[...] if off == 0 else q2h[off + reach]
            after[off] = keep * x + start[off] + coeff * around
        level2 = after

    own1 = [[x1p[pair, i] for i in range(half + 4)] for pair in range(pairs)]
    fixed = [[None] * (half + 4) for _ in range(pairs)]
    for off in (-1, 0, 1):
        wide = split_dot(level2[off], spread)
        for pair in range(pairs):
            view = t2.at[off + 1, pair]
            piece = wide[:, pair * zs:(pair + 1) * zs]
            view[pl.ds(0, y2, stride=2), :] = piece
            view[pl.ds(1, y2, stride=2), :] = piece
            for h in range(half):
                i = (off + 1) * half + h
                fixed[pair][i] = own1[pair][i] + view[...]
    for i in range(1, half + 3):
        coeff = q1h[0] if i == 1 else q1h[1] if i == half + 2 else q1s[i - 2]
        for pair in range(pairs):
            around = in_plane(fixed[pair][i], width1) + fixed[pair][i - 1] + fixed[pair][i + 1]
            smooth = keep * fixed[pair][i] + own1[pair][i] + coeff * around
            wide = split_dot(smooth, spread)
            w1[2 * pair, i - 1] = wide[:, :zs]
            w1[2 * pair + 1, i - 1] = wide[:, zs:]

    units = fields * planes
    share = units // group

    def correct(f):
        for i in range(half + 2):
            view = w0.at[i]
            piece = w1[f, i]
            view[pl.ds(0, y1, stride=2), :] = piece
            view[pl.ds(1, y1, stride=2), :] = piece
            wide = view[...]
            for slot in (2 * i - 1, 2 * i):
                if 0 <= slot <= planes + 1:
                    xp[f, slot] = xp[f, slot] + wide

    whole_fields = share % planes == 0
    if not whole_fields:
        for f in range(fields):
            correct(f)
    moves = [(dx, dc) for dx in range(group // 2 - 1, -1, -1) for dc in range(2)]
    moves = [m for m in moves if m != (0, 0)] + [(0, 0)]
    for index, (dx, dc) in enumerate(moves):
        owner = (v // 2 + dx) % (group // 2) * 2 + (v % 2 + dc) % 2
        if whole_fields:
            for i in range(share // planes):
                correct(owner * (share // planes) + i)
        for i in range(share):
            unit = owner * share + i
            f, p = unit // planes, unit % planes
            if whole_fields:
                f, p = owner * (share // planes) + i // planes, i % planes
            x = xp[f, p + 1]
            around = in_plane(x, zs) + xp[f, p] + xp[f, p + 2]
            result = keep * x + g0[p] * (rhs[0, f, p] + kap[p] * around)
            out[0, f, p] = result
            if (dx, dc) == (0, 0):
                zr[v, i] = result.astype(BF16)
            else:
                zb[index, i] = result.astype(BF16)
        if (dx, dc) != (0, 0):
            begin(None, zb.at[index], zr.at[v], sem_z + index, b, owner)
    for index, (dx, dc) in enumerate(moves):
        if (dx, dc) != (0, 0):
            source = (v // 2 + group // 2 - dx) % (group // 2) * 2 + (v % 2 + dc) % 2
            arrive(None, zr.at[source], sem_z + index)

    rows = 16
    keys = [(i, j) for i in range(group) for j in range(i, group)]
    per = ys // rows

    def products(step, totals):
        unit = step // per
        first = pl.multiple_of(step % per * rows, rows)
        values = [zr[i, unit, pl.ds(first, rows), :].astype(F32) for i in range(group)]
        return tuple(
            total + (values[i] * values[j]).reshape(rows // 8, 8, zs).sum(axis=0)
            for total, (i, j) in zip(totals, keys))

    totals = lax.fori_loop(0, share * per, products,
                           tuple(jnp.zeros((8, zs), F32) for _ in keys), unroll=4)
    part[...] = jnp.zeros_like(part)
    for (i, j), total in zip(keys, totals):
        line = jnp.sum(total, axis=0, keepdims=True)
        part[i, pl.ds(j, 1), :] = line
        if i != j:
            part[j, pl.ds(i, 1), :] = line
    for step in range(1, group):
        peer = (v + step) % group
        begin(None, part.at[peer], g1h.at[step], sem_g1 + step, b, peer)
    mine = part[v]
    for step in range(1, group):
        arrive(None, g1h.at[step], sem_g1 + step)
        mine = mine + g1h[step]
    rows_s[...] = mine
    for step in range(1, bricks):
        begin(None, rows_s, g2h.at[step], sem_g2 + step, (b + step) % bricks, v)
    for step in range(1, bricks):
        arrive(None, g2h.at[step], sem_g2 + step)
        mine = mine + g2h[step]
    sums = jnp.sum(mine, axis=1, keepdims=True)
    at_row = lax.broadcasted_iota(jnp.int32, mine.shape, 0)
    at_col = lax.broadcasted_iota(jnp.int32, mine.shape, 1)
    line = jnp.sum(jnp.where(at_row == at_col, sums, 0.0), axis=0, keepdims=True)
    gram[...] = line[:, :group]
    for cond, made in sends:
        if cond is None:
            made.wait_send()
        else:
            pl.when(cond)(made.wait_send)


def local(bricks, group, right_side, diffusivity):
    fields, planes, ys, zs = right_side.shape[1:]
    assert right_side.shape[0] == 1 and planes == 4 and zs == 128 and fields == 4
    pairs, half = fields // 2, planes // 2
    y1, y2 = ys // 2, ys // 4
    reach = min(SWEEPS, bricks - 1)
    units = fields * planes
    share = units // group
    tall = max(8, group)
    slots = 2 * reach + 1
    count = 2 * fields + 6 + 2 * slots + 2 * group + bricks
    vm = pltpu.VMEM
    return pl.pallas_call(
        functools.partial(kernel, bricks, group, reach),
        out_shape=(
            jax.ShapeDtypeStruct(right_side.shape, F32),
            jax.ShapeDtypeStruct((1, group), F32),
        ),
        in_specs=[pl.BlockSpec(memory_space=pltpu.VMEM)] * 2,
        out_specs=(pl.BlockSpec(memory_space=pltpu.VMEM),) * 2,
        scratch_shapes=[
            vm((fields, planes + 2, ys, zs), F32),
            vm((planes, ys, zs), F32),
            vm((2, fields, ys, zs), BF16),
            vm((2, fields, ys, zs), BF16),
            vm((fields, half, ys, zs), F32),
            vm((half, ys, zs), F32),
            vm((pairs, half + 4, y1, zs), F32),
            vm((half, pairs, y1, zs), F32),
            vm((2, half, pairs, y1, zs), F32),
            vm((pairs, half, y1, zs), F32),
            vm((half, y1, zs), F32),
            vm((half, y1, zs), F32),
            vm((2, y1, zs), F32),
            vm((pairs, y1, zs), F32),
            vm((y2, zs), F32),
            vm((slots, y2, zs), F32),
            vm((y2, zs), F32),
            vm((slots, y2, zs), F32),
            vm((3, pairs, y1, zs), F32),
            vm((fields, half + 2, y1, zs), F32),
            vm((half + 2, ys, zs), F32),
            vm((group, share, ys, zs), BF16),
            vm((group, share, ys, zs), BF16),
            vm((group, tall, zs), F32),
            vm((group, tall, zs), F32),
            vm((tall, zs), F32),
            vm((bricks, tall, zs), F32),
            pltpu.SemaphoreType.DMA((count,)),
            pltpu.SemaphoreType.DMA((count,)),
        ],
        compiler_params=pltpu.CompilerParams(
            collective_id=0, has_side_effects=True, vmem_limit_bytes=48 << 20
        ),
    )(right_side, diffusivity)


def solution(mesh):
    return jax.shard_map(
        functools.partial(local, mesh.shape["brick"], mesh.shape["vec"]),
        mesh=mesh,
        in_specs=(P("vec", None, "brick", None, None), P("brick", None, None)),
        out_specs=(P("vec", None, "brick", None, None), P("vec", None)),
        check_vma=False,
    )
```
